128 devices in a mesh: row: 8 (over z, y_lo), col: 16 (over x, y_hi, core).
Axes of the slice: x: 4, y: 4 (y_hi: 2, y_lo: 2; y = y_hi * 2 + y_lo), z: 4, core: 2. Of those that a mesh axis runs over, the one named last changes fastest.
Arguments:
- integrals: bfloat16 [10240, 10240], P('row', 'col'), may hold values from -6 to 6
- amplitudes: bfloat16 [10240, 8192], P('row', 'col'), may hold values from -0.0625 to 0.0625
- int_shape: int32 [40, 40], P('row'), may hold values 0 or 1
- amp_shape: int32 [40, 32], P(None, 'col'), may hold values 0 or 1
Outputs:
- ladder: bfloat16 [10240, 8192], P('row', 'col')
The draws below stay inside these ranges and needn't reach their ends.
All inputs are finite; a program needn't handle non-finite values. No bound on the sum of `int_shape` or of `amp_shape` on one device may be relied on, other than what follows from the above.
Results may differ from the reference program's by a relative error of at most 0.001.
Values may be sent and summed in bfloat16 or wider, within the bound.
No kernel may reach another device: no remote copies, remote signals or barrier semaphores. Data moves between devices by JAX's collectives and lax.ppermute only.
A program may use at most 192 MiB of HBM per device.

```python
import jax
import jax.numpy as jnp
from jax import lax

TILE = 256
ROW_TILES_DEV = 5
ROW_TILES = 40
K_TILES = 40
COL_TILES = 32
VROWS = 10240
OCOLS = 8192
KSUM = 10240
N_ROW = 8


def touch_ends(array, stream_key, smallest, largest):
    shape = array.shape
    spot = [jax.random.randint(jax.random.fold_in(stream_key, axis), (), 0, shape[axis]) for axis in range(len(shape))]
    array = array.at[tuple(spot)].set(smallest)
    longest = shape.index(max(shape))
    spot[longest] = (spot[longest] + 1) % shape[longest]
    return array.at[tuple(spot)].set(largest)


def levels(own_key, shape, shards, least, largest):
    level = 1.0
    for dim, shards_of in shards:
        steps = jax.random.uniform(jax.random.fold_in(jax.random.fold_in(own_key, 6), dim), (shards_of,), jnp.float32, least / len(shards), largest / len(shards))
        level = level * jnp.repeat(jnp.exp(steps), shape[dim] // shards_of).reshape((-1,) + (1,) * (len(shape) - 1 - dim))
    return level


def scatter_about(own_key, extent, width, reach, shards=(), kind=jnp.bfloat16):
    factor_of = levels(own_key, extent, shards, -0.22, 0.18) if shards else 1.0
    array = jax.random.normal(own_key, extent, jnp.float32) * width * factor_of
    return jnp.minimum(jnp.maximum(array, -reach), reach).astype(kind)


def setup_inputs(seed: int = 0) -> dict:
    key_list = jax.random.split(jax.random.key(seed), 5)
    integrals = scatter_about(key_list[0], (VROWS, KSUM), 1.0, 6.0, ((0, 8), (1, 16)))
    amplitudes = scatter_about(key_list[1], (KSUM, OCOLS), KSUM ** -0.5, 0.0625, ((0, 8), (1, 16)))
    int_shape = touch_ends((jax.random.randint(key_list[2], (ROW_TILES, K_TILES), 0, 3) < 2).astype(jnp.int32), jax.random.fold_in(key_list[2], 1), 0, 1)
    amp_shape = touch_ends((jax.random.randint(key_list[3], (K_TILES, COL_TILES), 0, 3) < 2).astype(jnp.int32), jax.random.fold_in(key_list[3], 1), 0, 1)
    return {"integrals": integrals, "amplitudes": amplitudes, "int_shape": int_shape, "amp_shape": amp_shape}


def expand_shape(shape_mask):
    return jnp.repeat(jnp.repeat(shape_mask, TILE, axis=0), TILE, axis=1).astype(jnp.bfloat16)


def reference(integrals, amplitudes, int_shape, amp_shape):
    masked_amp = amplitudes * expand_shape(amp_shape)
    row_blocks = integrals.reshape(N_ROW, ROW_TILES_DEV * TILE, K_TILES * TILE)
    shape_blocks = int_shape.reshape(N_ROW, ROW_TILES_DEV, K_TILES)

    def one_block(pair):
        block, shape_block = pair
        masked_int = block * expand_shape(shape_block)
        return jnp.dot(masked_int, masked_amp, preferred_element_type=jnp.float32).astype(jnp.bfloat16)

    ladder = lax.map(one_block, (row_blocks, shape_blocks))
    return ladder.reshape(N_ROW * ROW_TILES_DEV * TILE, masked_amp.shape[1])
```

```python
import functools

import jax
import jax.numpy as jnp
from jax import lax
from jax.experimental import pallas as pl
from jax.experimental.pallas import tpu as pltpu
from jax.sharding import Mesh, PartitionSpec as P

TILE = 256
AXES = ("z", "ylo", "x", "yhi", "core")
NX, NY, NZ = 4, 4, 4


def flat(z, y, x, c):
    z, y, x = z % NZ, y % NY, x % NX
    return (((z * 2 + y % 2) * NX + x) * 2 + y // 2) * 2 + c


def pairs_of(move):
    return [
        (flat(z, y, x, c), flat(*move(z, y, x, c)))
        for z in range(NZ)
        for y in range(NY)
        for x in range(NX)
        for c in range(2)
    ]


def sign(c):
    return 1 - 2 * c


X_AHEAD = pairs_of(lambda z, y, x, c: (z, y, x + sign(c), c))
X_BACK = pairs_of(lambda z, y, x, c: (z, y, x - sign(c), c))
Z_AHEAD = pairs_of(lambda z, y, x, c: (z + sign(c), y, x, c))
Z_BACK = pairs_of(lambda z, y, x, c: (z - sign(c), y, x, c))
Y_FAR = pairs_of(lambda z, y, x, c: (z, y + 2, x, c))
Y_NEAR = pairs_of(lambda z, y, x, c: (z, y ^ 1, x, c))
SWAP = pairs_of(lambda z, y, x, c: (z, y, x, 1 - c))


def send(value, pairs):
    return lax.ppermute(value, AXES, pairs)


def after(value, *earlier):
    return lax.optimization_barrier((value, *earlier))[0]


def mask_kernel(meta, amp_shape, b_ref, mine, other):
    chunk = TILE // 2
    count = mine.shape[0] // chunk
    for out, half in ((mine, meta[0]), (other, 1 - meta[0])):
        for i in range(count):
            source = half * count + i
            rows = pl.ds(pl.multiple_of(source * chunk, chunk), chunk)
            tile_row = meta[1] + source // 2
            for q in range(amp_shape.shape[1]):
                cols = pl.ds(q * TILE, TILE)
                value = b_ref[rows, cols]
                keep = amp_shape[tile_row, q] != 0
                out[pl.ds(i * chunk, chunk), cols] = jnp.where(keep, value, jnp.zeros_like(value))


def mask_halves(core, first, amp_shape, b):
    half = jax.ShapeDtypeStruct((b.shape[0] // 2, b.shape[1]), b.dtype)
    return pl.pallas_call(
        mask_kernel,
        out_shape=(half, half),
        in_specs=[pl.BlockSpec(memory_space=pltpu.SMEM)] * 2
        + [pl.BlockSpec(memory_space=pltpu.VMEM)],
        out_specs=[pl.BlockSpec(memory_space=pltpu.VMEM)] * 2,
        cost_estimate=pl.CostEstimate(flops=0, bytes_accessed=4 * b.size, transcendentals=0),
    )(jnp.stack([core, first]).astype(jnp.int32), amp_shape, b)


def block_kernel(n_groups, n_b, sides, has_acc, *refs):
    meta, int_shape = refs[:2]
    a_refs = refs[2 : 2 + n_groups]
    b_refs = refs[2 + n_groups : 2 + n_groups + n_b]
    rest = refs[2 + n_groups + n_b :]
    if has_acc:
        acc_in, rest = rest[0], rest[1:]
    out, a_buf, b_buf, acc, a_sem, b_sem, c_sem = rest
    slots, depth = a_buf.shape[0], a_buf.shape[2] // 2
    chunk = TILE // 2

    def a_copy(g):
        slot, part = g // 2 % slots, g % 2
        return pltpu.make_async_copy(
            a_refs[g], a_buf.at[slot, :, pl.ds(part * depth, depth)], a_sem.at[slot, part]
        )

    def b_copy(j, g):
        slot, part = g // 2 % slots, g % 2
        source = b_refs[j]
        if len(sides) == 1:
            source = source.at[pl.ds(sides[0], 1)]
        return pltpu.make_async_copy(
            source, b_buf.at[slot, :, pl.ds(part * depth, depth)], b_sem.at[slot, part]
        )

    def start(pair):
        for g in (2 * pair, 2 * pair + 1):
            for j in range(n_b):
                @pl.when(meta[1 + n_groups + j] == meta[1 + g])
                def _():
                    b_copy(j, g).start()
            a_copy(g).start()

    pairs = n_groups // 2
    for pair in range(min(slots, pairs)):
        start(pair)
    if has_acc:
        source = acc_in.at[pl.ds(sides[0], 1)] if len(sides) == 1 else acc_in
        acc_copy = pltpu.make_async_copy(source, acc, c_sem)
        acc_copy.start()
        acc_copy.wait()

    for pair in range(pairs):
        slot = pair % slots
        for g in (2 * pair, 2 * pair + 1):
            b_copy(0, g).wait()
            a_copy(g).wait()
        first = [(2 * meta[1 + g] + meta[0]) * (depth // chunk) for g in (2 * pair, 2 * pair + 1)]
        for p in range(int_shape.shape[0]):
            rows = pl.ds(p * TILE, TILE)
            parts = []
            for h in range(2):
                for j in range(depth // chunk):
                    value = a_buf[slot, rows, pl.ds(h * depth + j * chunk, chunk)]
                    keep = int_shape[p, (first[h] + j) // 2] != 0
                    parts.append(jnp.where(keep, value, jnp.zeros_like(value)))
            left = jnp.concatenate(parts, axis=1)
            for i in range(len(sides)):
                total = jnp.dot(left, b_buf[slot, i], preferred_element_type=jnp.float32)
                if pair > 0 or has_acc:
                    total = total + acc[i, rows, :]
                acc[i, rows, :] = total
        if pair + slots < pairs:
            start(pair + slots)
    out_copy = pltpu.make_async_copy(acc, out, c_sem)
    out_copy.start()
    out_copy.wait()


def block_matmul(core, int_shape, groups, b_blocks, sides, acc=None):
    a_refs, a_of = [g[0] for g in groups], [g[1] for g in groups]
    b_refs, b_of = [b[0] for b in b_blocks], [b[1] for b in b_blocks]
    rows, depth = a_refs[0].shape
    columns = b_refs[0].shape[2]
    n = len(groups)
    slots = min(2, n // 2)
    meta = jnp.stack([core] + a_of + b_of).astype(jnp.int32)
    operands = [meta, int_shape] + a_refs + b_refs + ([] if acc is None else [acc])
    in_specs = [pl.BlockSpec(memory_space=pltpu.SMEM)] * 2
    in_specs += [pl.BlockSpec(memory_space=pltpu.HBM)] * (len(operands) - 2)
    return pl.pallas_call(
        functools.partial(block_kernel, n, len(b_refs), sides, acc is not None),
        out_shape=jax.ShapeDtypeStruct((len(sides), rows, columns), jnp.float32),
        in_specs=in_specs,
        out_specs=pl.BlockSpec(memory_space=pltpu.HBM),
        scratch_shapes=[
            pltpu.VMEM((slots, rows, 2 * depth), jnp.bfloat16),
            pltpu.VMEM((slots, len(sides), 2 * depth, columns), jnp.bfloat16),
            pltpu.VMEM((len(sides), rows, columns), jnp.float32),
            pltpu.SemaphoreType.DMA((slots, 2)),
            pltpu.SemaphoreType.DMA((slots, 2)),
            pltpu.SemaphoreType.DMA,
        ],
        cost_estimate=pl.CostEstimate(
            flops=2 * rows * depth * columns * n * len(sides),
            bytes_accessed=n * 2 * depth * (rows + len(sides) * columns),
            transcendentals=0,
        ),
    )(*operands)


def per_device(a, b, int_shape, amp_shape):
    z, ylo, x = lax.axis_index("z"), lax.axis_index("ylo"), lax.axis_index("x")
    yhi, core = lax.axis_index("yhi"), lax.axis_index("core")
    step = sign(core)
    barrier = lax.optimization_barrier

    x1 = send(a, X_AHEAD)
    x2 = send(a, X_BACK)
    aq = send(a, Y_FAR)
    mine, other = mask_halves(core, (2 * z + ylo) * (b.shape[0] // TILE), amp_shape, b)
    b0 = jnp.stack([mine, send(other, SWAP)])
    z1 = send(b0, Z_AHEAD)
    z2 = send(b0, Z_BACK)
    a0, b0, x1, x2, aq, z1, z2 = barrier((a, b0, x1, x2, aq, z1, z2))

    x3 = send(x1, X_AHEAD)
    x4 = send(aq, X_AHEAD)
    z3 = send(z1, Z_AHEAD)
    bq = send(b0, Y_NEAR)
    b0, aq, x3, x4, z3, bq = barrier((b0, aq, x3, x4, z3, bq))

    x5 = send(aq, X_BACK)
    x6 = send(x4, X_AHEAD)
    z4 = send(bq, Z_AHEAD)
    z5 = send(bq, Z_BACK)
    z6 = send(z3, Y_NEAR)

    spots = [x, (x - step) % NX, (x + step) % NX, (x + 2) % NX]
    group_of = [2 * s + yhi for s in spots] + [2 * s + 1 - yhi for s in spots]
    groups = list(zip([a0, x1, x2, x3, aq, x4, x5, x6], group_of))
    deep = [z, (z - step) % NZ, (z + step) % NZ, (z + 2) % NZ]
    b_of = [2 * s + ylo for s in deep] + [2 * s + 1 - ylo for s in deep]
    b_blocks = list(zip([b0, z1, z2, z3, bq, z4, z5, z6], b_of))

    early = block_matmul(core, int_shape, groups[:6], b_blocks, (0, 1))
    theirs = block_matmul(core, int_shape, groups[6:], b_blocks, (1,), early)
    got = send(theirs, SWAP)
    ours = block_matmul(core, int_shape, groups[6:], b_blocks, (0,), early)
    return (ours + got)[0].astype(jnp.bfloat16)


def solution(mesh):
    fine = Mesh(mesh.devices.reshape(NZ, 2, NX, 2, 2), AXES)
    row, col = ("z", "ylo"), ("x", "yhi", "core")
    return jax.shard_map(
        per_device,
        mesh=fine,
        in_specs=(P(row, col), P(row, col), P(row, None), P(None, col)),
        out_specs=P(row, col),
        check_vma=False,
    )
```

```python
import functools

import jax
import jax.numpy as jnp
from jax import lax
from jax.experimental import pallas as pl
from jax.experimental.pallas import tpu as pltpu
from jax.sharding import Mesh, PartitionSpec as P

TILE = 256
AXES = ("z", "ylo", "x", "yhi", "core")
NX, NY, NZ = 4, 4, 4


def flat(z, y, x, c):
    z, y, x = z % NZ, y % NY, x % NX
    return (((z * 2 + y % 2) * NX + x) * 2 + y // 2) * 2 + c


def pairs_of(move):
    return [
        (flat(z, y, x, c), flat(*move(z, y, x, c)))
        for z in range(NZ)
        for y in range(NY)
        for x in range(NX)
        for c in range(2)
    ]


def sign(c):
    return 1 - 2 * c


X_AHEAD = pairs_of(lambda z, y, x, c: (z, y, x + sign(c), c))
X_BACK = pairs_of(lambda z, y, x, c: (z, y, x - sign(c), c))
Z_AHEAD = pairs_of(lambda z, y, x, c: (z + sign(c), y, x, c))
Z_BACK = pairs_of(lambda z, y, x, c: (z - sign(c), y, x, c))
Y_FAR = pairs_of(lambda z, y, x, c: (z, y + 2, x, c))
Y_NEAR = pairs_of(lambda z, y, x, c: (z, y ^ 1, x, c))
SWAP = pairs_of(lambda z, y, x, c: (z, y, x, 1 - c))


def send(value, pairs):
    return lax.ppermute(value, AXES, pairs)


def after(value, *earlier):
    return lax.optimization_barrier((value, *earlier))[0]


CHUNK = TILE // 2


def mask_kernel(meta, own_shape, next_shape, own, following, out, buffer, sems):
    core, first = meta[0], meta[1]
    half = buffer.shape[1]
    rows = pl.ds(pl.multiple_of(core * half, half), half)
    copies = [
        pltpu.make_async_copy(source.at[rows], buffer.at[side], sems.at[side])
        for side, source in enumerate((own, following))
    ]
    for copy in copies:
        copy.start()
    for side, shape in enumerate((own_shape, next_shape)):
        copies[side].wait()
        for i in range(half // CHUNK):
            chunk = pl.ds(i * CHUNK, CHUNK)
            tile_row = first + (core * (half // CHUNK) + i) // 2
            for q in range(shape.shape[0]):
                cols = pl.ds(q * TILE, TILE)
                value = buffer[side, chunk, cols]
                value = jnp.where(shape[q, tile_row] != 0, value, jnp.zeros_like(value))
                out[side, chunk, cols] = value


def masked_half(meta, own_shape, next_shape, own, following):
    half = (own.shape[0] // 2, own.shape[1])
    return pl.pallas_call(
        mask_kernel,
        out_shape=jax.ShapeDtypeStruct((2, *half), own.dtype),
        in_specs=[pl.BlockSpec(memory_space=pltpu.SMEM)] * 3
        + [pl.BlockSpec(memory_space=pltpu.HBM)] * 2,
        out_specs=pl.BlockSpec(memory_space=pltpu.VMEM),
        scratch_shapes=[pltpu.VMEM((2, *half), own.dtype), pltpu.SemaphoreType.DMA((2,))],
        cost_estimate=pl.CostEstimate(flops=0, bytes_accessed=4 * own.size, transcendentals=0),
    )(meta, own_shape, next_shape, own, following)


def block_kernel(spots, b_spots, b_from, plan, sides, has_acc, *refs):
    n_groups, n_sides = len(spots), len(sides)
    n_b = 1 + max(max(pick) for pick in b_from)
    meta, int_shape = refs[:2]
    a_refs = refs[2 : 2 + n_groups]
    b_refs = refs[2 + n_groups : 2 + n_groups + n_b]
    rest = refs[2 + n_groups + n_b :]
    acc_ins = ()
    if has_acc:
        acc_ins, rest = rest[:n_sides], rest[n_sides:]
    outs, rest = rest[:n_sides], rest[n_sides:]
    a_buf, b_buf, acc, a_sem, b_sem, in_sem, out_sem = rest
    depth = a_buf.shape[3]
    row_tiles = int_shape.shape[0]
    strips = ((0, 1), (1, 3), (3, 4), (4, row_tiles))
    window = 2
    followers = {next_pair for _, _, _, next_pair in plan}

    def rows_of(s):
        return pl.ds(strips[s][0] * TILE, (strips[s][1] - strips[s][0]) * TILE)

    def members(pair):
        return (2 * pair, 2 * pair + 1)

    def a_copy(g, s):
        slot, part = plan[g // 2][1], g % 2
        return pltpu.make_async_copy(
            a_refs[g].at[rows_of(s)], a_buf.at[slot, part, rows_of(s)], a_sem.at[slot, part, s]
        )

    def b_copy(j, g, i):
        slot, part = plan[g // 2][1], g % 2
        source = b_refs[b_from[j][sides[i]]]
        if len(source.shape) == 3:
            source = source.at[sides[i]]
        return pltpu.make_async_copy(
            source, b_buf.at[slot, i, pl.ds(part * depth, depth)], b_sem.at[slot, part, i]
        )

    def acc_copy(i, s):
        return pltpu.make_async_copy(
            acc_ins[i].at[rows_of(s)], acc.at[i, rows_of(s)], in_sem.at[i, s]
        )

    def out_copy(i, s):
        return pltpu.make_async_copy(
            acc.at[i, rows_of(s)], outs[i].at[rows_of(s)], out_sem.at[i, s]
        )

    def fetch(pair, s):
        for g in members(pair):
            a_copy(g, s).start()
        if has_acc and pair not in followers:
            for i in range(n_sides):
                acc_copy(i, s).start()

    def begin(pair):
        for g in members(pair):
            for j in range(len(b_spots)):
                @pl.when(meta[b_spots[j]] == meta[spots[g]])
                def _():
                    for i in range(n_sides):
                        b_copy(j, g, i).start()
        for s in range(window):
            fetch(pair, s)

    def guarded(pair, work):
        flag = plan[pair][0]
        if flag is None:
            work()
        else:
            pl.when(meta[1] == flag)(work)

    for pair in range(len(plan)):
        if pair not in followers:
            guarded(pair, functools.partial(begin, pair))

    def multiply(pair):
        _, slot, last, next_pair = plan[pair]
        for g in members(pair):
            for i in range(n_sides):
                b_copy(0, g, i).wait()
        first = [(2 * meta[spots[g]] + meta[0]) * (depth // CHUNK) for g in members(pair)]
        for s in range(len(strips)):
            for g in members(pair):
                a_copy(g, s).wait()
            if has_acc and pair not in followers:
                for i in range(n_sides):
                    acc_copy(i, s).wait()
            if s + window < len(strips):
                fetch(pair, s + window)
            elif s + window == len(strips) and next_pair is not None:
                begin(next_pair)
            for p in range(*strips[s]):
                rows = pl.ds(p * TILE, TILE)
                parts = []
                for h in range(2):
                    for j in range(depth // CHUNK):
                        value = a_buf[slot, h, rows, pl.ds(j * CHUNK, CHUNK)]
                        keep = int_shape[p, (first[h] + j) // 2] != 0
                        parts.append(jnp.where(keep, value, jnp.zeros_like(value)))
                left = jnp.concatenate(parts, axis=1)
                for i in range(n_sides):
                    total = jnp.dot(left, b_buf[slot, i], preferred_element_type=jnp.float32)
                    if has_acc or pair in followers:
                        total = total + acc[i, rows, :]
                    acc[i, rows, :] = total
            if last:
                for i in range(n_sides):
                    out_copy(i, s).start()

    for pair in range(len(plan)):
        guarded(pair, functools.partial(multiply, pair))
    for s in range(len(strips)):
        for i in range(n_sides):
            out_copy(i, s).wait()


def block_matmul(meta, int_shape, groups, b_blocks, sides, plan, weight, accs=()):
    a_refs, spots = [g[0] for g in groups], tuple(g[1] for g in groups)
    b_refs, b_from, b_spots = [], [], []
    for block, spot in b_blocks:
        many = isinstance(block, tuple)
        b_from.append((len(b_refs), len(b_refs) + int(many)))
        b_refs.extend(block if many else (block,))
        b_spots.append(spot)
    rows, depth = a_refs[0].shape
    columns = b_refs[0].shape[-1]
    m = len(sides)
    operands = [meta, int_shape] + a_refs + b_refs + list(accs)
    in_specs = [pl.BlockSpec(memory_space=pltpu.SMEM)] * 2
    in_specs += [pl.BlockSpec(memory_space=pltpu.HBM)] * (len(operands) - 2)
    return pl.pallas_call(
        functools.partial(
            block_kernel, spots, tuple(b_spots), tuple(b_from), plan, sides, bool(accs)
        ),
        out_shape=(jax.ShapeDtypeStruct((rows, columns), jnp.float32),) * m,
        in_specs=in_specs,
        out_specs=(pl.BlockSpec(memory_space=pltpu.HBM),) * m,
        scratch_shapes=[
            pltpu.VMEM((2, 2, rows, depth), jnp.bfloat16),
            pltpu.VMEM((2, m, 2 * depth, columns), jnp.bfloat16),
            pltpu.VMEM((m, rows, columns), jnp.float32),
            pltpu.SemaphoreType.DMA((2, 2, 4)),
            pltpu.SemaphoreType.DMA((2, 2, m)),
            pltpu.SemaphoreType.DMA((m, 4)),
            pltpu.SemaphoreType.DMA((m, 4)),
        ],
        cost_estimate=pl.CostEstimate(
            flops=weight * 2 * rows * depth * columns,
            bytes_accessed=2 * rows * depth,
            transcendentals=0,
        ),
    )(*operands)


def per_device(a, b, int_shape, amp_shape):
    z, ylo, x = lax.axis_index("z"), lax.axis_index("ylo"), lax.axis_index("x")
    yhi, core = lax.axis_index("yhi"), lax.axis_index("core")
    step = sign(core)
    barrier = lax.optimization_barrier

    spots = [x, (x - step) % NX, (x + step) % NX, (x + 2) % NX]
    deep = [z, (z - step) % NZ, (z + step) % NZ, (z + 2) % NZ]
    meta = [core, (ylo == yhi).astype(jnp.int32)]
    meta += [2 * s + yhi for s in spots] + [2 * s + 1 - yhi for s in spots]
    meta += [2 * s + ylo for s in deep] + [2 * s + 1 - ylo for s in deep]
    meta = jnp.stack(meta).astype(jnp.int32)
    first = jnp.stack([core, (2 * z + ylo) * (b.shape[0] // TILE)]).astype(jnp.int32)

    x1 = send(a, X_AHEAD)
    x2 = send(a, X_BACK)
    aq = send(a, Y_FAR)
    shape_t = amp_shape.T
    b0 = masked_half(first, shape_t, send(shape_t, SWAP), b, send(b, SWAP))
    z1 = send(b0, Z_AHEAD)
    z2 = send(b0, Z_BACK)
    x3 = send(x1, X_AHEAD)
    x5 = send(after(aq, x2), X_BACK)
    z3 = send(z1, Z_AHEAD)
    q = send(after(b0, aq, z2), Y_NEAR)
    x4 = send(after(aq, x3), X_AHEAD)
    x6 = send(x5, X_BACK)
    z4 = send(after(q, z3), Z_AHEAD)
    z5 = send(after(q, z3), Z_BACK)
    z6 = send(after(z3, q), Y_NEAR)

    a_blocks = [a, x1, x2, x3, aq, x4, x5, x6]
    groups = [(block, 2 + i) for i, block in enumerate(a_blocks)]
    near = [(block, 10 + i) for i, block in enumerate([b0, z1, z2, z3])]
    far = [(block, 14 + i) for i, block in enumerate([q, z4, z5, z6])]
    ready = groups[:4] + [groups[4], groups[6]]
    near_plan = ((1, 0, False, 1), (1, 1, True, None), (0, 0, True, None))
    far_plan = ((0, 0, False, 1), (0, 1, True, None), (1, 0, True, None))
    sums = block_matmul(meta, int_shape, ready, near, (0, 1), near_plan, 2)
    sums = block_matmul(meta, int_shape, ready, far, (0, 1), far_plan, 6, sums)
    late, late_plan = [groups[5], groups[7]], ((None, 0, True, None),)
    theirs = block_matmul(meta, int_shape, late, near + far, (1,), late_plan, 1, sums[1:])[0]
    got = send(theirs, SWAP)
    ours = block_matmul(meta, int_shape, late, near + far, (0,), late_plan, 1, sums[:1])[0]
    return (ours + got).astype(jnp.bfloat16)


def solution(mesh):
    fine = Mesh(mesh.devices.reshape(NZ, 2, NX, 2, 2), AXES)
    row, col = ("z", "ylo"), ("x", "yhi", "core")
    return jax.shard_map(
        per_device,
        mesh=fine,
        in_specs=(P(row, col), P(row, col), P(row, None), P(None, col)),
        out_specs=P(row, col),
        check_vma=False,
    )
```

```python
import functools

import jax
import jax.numpy as jnp
from jax import lax
from jax.experimental import pallas as pl
from jax.experimental.pallas import tpu as pltpu
from jax.sharding import Mesh, PartitionSpec as P

TILE = 256
AXES = ("z", "ylo", "x", "yhi", "core")
NX, NY, NZ = 4, 4, 4


def flat(z, y, x, c):
    z, y, x = z % NZ, y % NY, x % NX
    return (((z * 2 + y % 2) * NX + x) * 2 + y // 2) * 2 + c


def pairs_of(move):
    return [
        (flat(z, y, x, c), flat(*move(z, y, x, c)))
        for z in range(NZ)
        for y in range(NY)
        for x in range(NX)
        for c in range(2)
    ]


def sign(c):
    return 1 - 2 * c


X_AHEAD = pairs_of(lambda z, y, x, c: (z, y, x + sign(c), c))
X_BACK = pairs_of(lambda z, y, x, c: (z, y, x - sign(c), c))
Z_AHEAD = pairs_of(lambda z, y, x, c: (z + sign(c), y, x, c))
Z_BACK = pairs_of(lambda z, y, x, c: (z - sign(c), y, x, c))
Y_FAR = pairs_of(lambda z, y, x, c: (z, y + 2, x, c))
Y_NEAR = pairs_of(lambda z, y, x, c: (z, y ^ 1, x, c))
SWAP = pairs_of(lambda z, y, x, c: (z, y, x, 1 - c))


def send(value, pairs):
    return lax.ppermute(value, AXES, pairs)


def after(value, *earlier):
    return lax.optimization_barrier((value, *earlier))[0]


CHUNK = TILE // 2


def mask_kernel(meta, own_shape, next_shape, own, following, out, buffer, sems):
    core, first = meta[0], meta[1]
    half = buffer.shape[1]
    rows = pl.ds(pl.multiple_of(core * half, half), half)
    copies = [
        pltpu.make_async_copy(source.at[rows], buffer.at[side], sems.at[side])
        for side, source in enumerate((own, following))
    ]
    for copy in copies:
        copy.start()
    for side, shape in enumerate((own_shape, next_shape)):
        copies[side].wait()
        for i in range(half // CHUNK):
            chunk = pl.ds(i * CHUNK, CHUNK)
            tile_row = first + (core * (half // CHUNK) + i) // 2
            for q in range(shape.shape[0]):
                cols = pl.ds(q * TILE, TILE)
                value = buffer[side, chunk, cols]
                value = jnp.where(shape[q, tile_row] != 0, value, jnp.zeros_like(value))
                out[side, chunk, cols] = value


def masked_half(meta, own_shape, next_shape, own, following):
    half = (own.shape[0] // 2, own.shape[1])
    return pl.pallas_call(
        mask_kernel,
        out_shape=jax.ShapeDtypeStruct((2, *half), own.dtype),
        in_specs=[pl.BlockSpec(memory_space=pltpu.SMEM)] * 3
        + [pl.BlockSpec(memory_space=pltpu.HBM)] * 2,
        out_specs=pl.BlockSpec(memory_space=pltpu.VMEM),
        scratch_shapes=[pltpu.VMEM((2, *half), own.dtype), pltpu.SemaphoreType.DMA((2,))],
        cost_estimate=pl.CostEstimate(flops=0, bytes_accessed=4 * own.size, transcendentals=0),
    )(meta, own_shape, next_shape, own, following)


def block_kernel(spots, b_spots, b_from, plan, sides, has_acc, *refs):
    n_groups, n_sides = len(spots), len(sides)
    n_b = 1 + max(max(pick) for pick in b_from)
    meta, int_shape = refs[:2]
    a_refs = refs[2 : 2 + n_groups]
    b_refs = refs[2 + n_groups : 2 + n_groups + n_b]
    rest = refs[2 + n_groups + n_b :]
    acc_ins = ()
    if has_acc:
        acc_ins, rest = rest[:n_sides], rest[n_sides:]
    outs, rest = rest[:n_sides], rest[n_sides:]
    a_buf, b_buf, acc, a_sem, b_sem, in_sem, out_sem = rest
    depth = a_buf.shape[3]
    row_tiles = int_shape.shape[0]
    strips = ((0, 1), (1, 3), (3, 4), (4, row_tiles))
    window = 2
    followers = {next_pair for _, _, _, next_pair in plan}

    def rows_of(s):
        return pl.ds(strips[s][0] * TILE, (strips[s][1] - strips[s][0]) * TILE)

    def members(pair):
        return (2 * pair, 2 * pair + 1)

    def a_copy(g, s):
        slot, part = plan[g // 2][1], g % 2
        return pltpu.make_async_copy(
            a_refs[g].at[rows_of(s)], a_buf.at[slot, part, rows_of(s)], a_sem.at[slot, part, s]
        )

    def b_copy(j, g, i):
        slot, part = plan[g // 2][1], g % 2
        source = b_refs[b_from[j][sides[i]]]
        if len(source.shape) == 3:
            source = source.at[sides[i]]
        return pltpu.make_async_copy(
            source, b_buf.at[slot, i, pl.ds(part * depth, depth)], b_sem.at[slot, part, i]
        )

    def acc_copy(i, s):
        return pltpu.make_async_copy(
            acc_ins[i].at[rows_of(s)], acc.at[i, rows_of(s)], in_sem.at[i, s]
        )

    def out_copy(i, s):
        return pltpu.make_async_copy(
            acc.at[i, rows_of(s)], outs[i].at[rows_of(s)], out_sem.at[i, s]
        )

    def fetch(pair, s):
        for g in members(pair):
            a_copy(g, s).start()
        if has_acc and pair not in followers:
            for i in range(n_sides):
                acc_copy(i, s).start()

    def begin(pair):
        for g in members(pair):
            for j in range(len(b_spots)):
                @pl.when(meta[b_spots[j]] == meta[spots[g]])
                def _():
                    for i in range(n_sides):
                        b_copy(j, g, i).start()
        for s in range(window):
            fetch(pair, s)

    def guarded(pair, work):
        flag = plan[pair][0]
        if flag is None:
            work()
        else:
            pl.when(meta[1] == flag)(work)

    for pair in range(len(plan)):
        if pair not in followers:
            guarded(pair, functools.partial(begin, pair))

    def multiply(pair):
        _, slot, last, next_pair = plan[pair]
        for g in members(pair):
            for i in range(n_sides):
                b_copy(0, g, i).wait()
        first = [(2 * meta[spots[g]] + meta[0]) * (depth // CHUNK) for g in members(pair)]
        for s in range(len(strips)):
            for g in members(pair):
                a_copy(g, s).wait()
            if has_acc and pair not in followers:
                for i in range(n_sides):
                    acc_copy(i, s).wait()
            if s + window < len(strips):
                fetch(pair, s + window)
            elif s + window == len(strips) and next_pair is not None:
                begin(next_pair)
            for p in range(*strips[s]):
                rows = pl.ds(p * TILE, TILE)
                parts = []
                for h in range(2):
                    for j in range(depth // CHUNK):
                        value = a_buf[slot, h, rows, pl.ds(j * CHUNK, CHUNK)]
                        keep = int_shape[p, (first[h] + j) // 2] != 0
                        parts.append(jnp.where(keep, value, jnp.zeros_like(value)))
                left = jnp.concatenate(parts, axis=1)
                for i in range(n_sides):
                    total = jnp.dot(left, b_buf[slot, i], preferred_element_type=jnp.float32)
                    if has_acc or pair in followers:
                        total = total + acc[i, rows, :]
                    acc[i, rows, :] = total
            if last:
                for i in range(n_sides):
                    out_copy(i, s).start()

    for pair in range(len(plan)):
        guarded(pair, functools.partial(multiply, pair))
    for s in range(len(strips)):
        for i in range(n_sides):
            out_copy(i, s).wait()


def block_matmul(meta, int_shape, groups, b_blocks, sides, plan, weight, accs=()):
    a_refs, spots = [g[0] for g in groups], tuple(g[1] for g in groups)
    b_refs, b_from, b_spots = [], [], []
    for block, spot in b_blocks:
        many = isinstance(block, tuple)
        b_from.append((len(b_refs), len(b_refs) + int(many)))
        b_refs.extend(block if many else (block,))
        b_spots.append(spot)
    rows, depth = a_refs[0].shape
    columns = b_refs[0].shape[-1]
    m = len(sides)
    operands = [meta, int_shape] + a_refs + b_refs + list(accs)
    in_specs = [pl.BlockSpec(memory_space=pltpu.SMEM)] * 2
    in_specs += [pl.BlockSpec(memory_space=pltpu.HBM)] * (len(operands) - 2)
    return pl.pallas_call(
        functools.partial(
            block_kernel, spots, tuple(b_spots), tuple(b_from), plan, sides, bool(accs)
        ),
        out_shape=(jax.ShapeDtypeStruct((rows, columns), jnp.float32),) * m,
        in_specs=in_specs,
        out_specs=(pl.BlockSpec(memory_space=pltpu.HBM),) * m,
        scratch_shapes=[
            pltpu.VMEM((2, 2, rows, depth), jnp.bfloat16),
            pltpu.VMEM((2, m, 2 * depth, columns), jnp.bfloat16),
            pltpu.VMEM((m, rows, columns), jnp.float32),
            pltpu.SemaphoreType.DMA((2, 2, 4)),
            pltpu.SemaphoreType.DMA((2, 2, m)),
            pltpu.SemaphoreType.DMA((m, 4)),
            pltpu.SemaphoreType.DMA((m, 4)),
        ],
        cost_estimate=pl.CostEstimate(
            flops=weight * 2 * rows * depth * columns,
            bytes_accessed=2 * rows * depth,
            transcendentals=0,
        ),
    )(*operands)


def per_device(a, b, int_shape, amp_shape):
    z, ylo, x = lax.axis_index("z"), lax.axis_index("ylo"), lax.axis_index("x")
    yhi, core = lax.axis_index("yhi"), lax.axis_index("core")
    step = sign(core)
    barrier = lax.optimization_barrier

    spots = [x, (x - step) % NX, (x + step) % NX, (x + 2) % NX]
    deep = [z, (z - step) % NZ, (z + step) % NZ, (z + 2) % NZ]
    meta = [core, (ylo == yhi).astype(jnp.int32)]
    meta += [2 * s + yhi for s in spots] + [2 * s + 1 - yhi for s in spots]
    meta += [2 * s + ylo for s in deep] + [2 * s + 1 - ylo for s in deep]
    meta = jnp.stack(meta).astype(jnp.int32)
    first = jnp.stack([core, (2 * z + ylo) * (b.shape[0] // TILE)]).astype(jnp.int32)

    x1 = send(a, X_AHEAD)
    x2 = send(a, X_BACK)
    aq = send(a, Y_FAR)
    shape_t = amp_shape.T
    b0 = masked_half(first, shape_t, send(shape_t, SWAP), b, send(b, SWAP))
    z1 = send(b0, Z_AHEAD)
    z2 = send(b0, Z_BACK)
    q = send(after(b0, x1), Y_NEAR)
    x3 = send(x1, X_AHEAD)
    x5 = send(after(aq, x2), X_BACK)
    z3 = send(after(z1, z2), Z_AHEAD)
    x4 = send(after(aq, x3), X_AHEAD)
    x6 = send(x5, X_BACK)
    z4 = send(after(q, z3), Z_AHEAD)
    z5 = send(after(q, z3), Z_BACK)
    z6 = send(after(z3, q), Y_NEAR)

    a_blocks = [a, x1, x2, x3, aq, x4, x5, x6]
    groups = [(block, 2 + i) for i, block in enumerate(a_blocks)]
    near = [(block, 10 + i) for i, block in enumerate([b0, z1, z2, z3])]
    far = [(block, 14 + i) for i, block in enumerate([q, z4, z5, z6])]
    ready = groups[:4] + [groups[4], groups[6]]
    near_plan = ((1, 0, False, 1), (1, 1, True, None), (0, 0, True, None))
    far_plan = ((0, 0, False, 1), (0, 1, True, None), (1, 0, True, None))
    sums = block_matmul(meta, int_shape, ready, near, (0, 1), near_plan, 2)
    sums = block_matmul(meta, int_shape, ready, far, (0, 1), far_plan, 7, sums)
    late, late_plan = [groups[5], groups[7]], ((None, 0, True, None),)
    theirs = block_matmul(meta, int_shape, late, near + far, (1,), late_plan, 1, sums[1:])[0]
    got = send(theirs, SWAP)
    ours = block_matmul(meta, int_shape, late, near + far, (0,), late_plan, 1, sums[:1])[0]
    return (ours + got).astype(jnp.bfloat16)


def solution(mesh):
    fine = Mesh(mesh.devices.reshape(NZ, 2, NX, 2, 2), AXES)
    row, col = ("z", "ylo"), ("x", "yhi", "core")
    return jax.shard_map(
        per_device,
        mesh=fine,
        in_specs=(P(row, col), P(row, col), P(row, None), P(None, col)),
        out_specs=P(row, col),
        check_vma=False,
    )
```

```python
import functools

import jax
import jax.numpy as jnp
from jax import lax
from jax.experimental import pallas as pl
from jax.experimental.pallas import tpu as pltpu
from jax.sharding import Mesh, PartitionSpec as P

TILE = 256
AXES = ("z", "ylo", "x", "yhi", "core")
NX, NY, NZ = 4, 4, 4


def flat(z, y, x, c):
    z, y, x = z % NZ, y % NY, x % NX
    return (((z * 2 + y % 2) * NX + x) * 2 + y // 2) * 2 + c


def pairs_of(move):
    return [
        (flat(z, y, x, c), flat(*move(z, y, x, c)))
        for z in range(NZ)
        for y in range(NY)
        for x in range(NX)
        for c in range(2)
    ]


def sign(c):
    return 1 - 2 * c


X_AHEAD = pairs_of(lambda z, y, x, c: (z, y, x + sign(c), c))
X_BACK = pairs_of(lambda z, y, x, c: (z, y, x - sign(c), c))
Z_AHEAD = pairs_of(lambda z, y, x, c: (z + sign(c), y, x, c))
Z_BACK = pairs_of(lambda z, y, x, c: (z - sign(c), y, x, c))
Y_FAR = pairs_of(lambda z, y, x, c: (z, y + 2, x, c))
Y_NEAR = pairs_of(lambda z, y, x, c: (z, y ^ 1, x, c))
SWAP = pairs_of(lambda z, y, x, c: (z, y, x, 1 - c))


def send(value, pairs):
    return lax.ppermute(value, AXES, pairs)


def after(value, *earlier):
    return lax.optimization_barrier((value, *earlier))[0]


CHUNK = TILE // 2


def mask_kernel(meta, own_shape, next_shape, own, following, out, buffer, sems):
    core, first = meta[0], meta[1]
    half = buffer.shape[1]
    rows = pl.ds(pl.multiple_of(core * half, half), half)
    copies = [
        pltpu.make_async_copy(source.at[rows], buffer.at[side], sems.at[side])
        for side, source in enumerate((own, following))
    ]
    for copy in copies:
        copy.start()
    for side, shape in enumerate((own_shape, next_shape)):
        copies[side].wait()
        for i in range(half // CHUNK):
            chunk = pl.ds(i * CHUNK, CHUNK)
            tile_row = first + (core * (half // CHUNK) + i) // 2
            for q in range(shape.shape[0]):
                cols = pl.ds(q * TILE, TILE)
                value = buffer[side, chunk, cols]
                value = jnp.where(shape[q, tile_row] != 0, value, jnp.zeros_like(value))
                out[side, chunk, cols] = value


def masked_half(meta, own_shape, next_shape, own, following):
    half = (own.shape[0] // 2, own.shape[1])
    return pl.pallas_call(
        mask_kernel,
        out_shape=jax.ShapeDtypeStruct((2, *half), own.dtype),
        in_specs=[pl.BlockSpec(memory_space=pltpu.SMEM)] * 3
        + [pl.BlockSpec(memory_space=pltpu.HBM)] * 2,
        out_specs=pl.BlockSpec(memory_space=pltpu.VMEM),
        scratch_shapes=[pltpu.VMEM((2, *half), own.dtype), pltpu.SemaphoreType.DMA((2,))],
        cost_estimate=pl.CostEstimate(flops=0, bytes_accessed=4 * own.size, transcendentals=0),
    )(meta, own_shape, next_shape, own, following)


def block_kernel(spots, b_spots, b_from, plan, sides, has_acc, *refs):
    n_groups, n_sides = len(spots), len(sides)
    n_b = 1 + max(max(pick) for pick in b_from)
    meta, int_shape = refs[:2]
    a_refs = refs[2 : 2 + n_groups]
    b_refs = refs[2 + n_groups : 2 + n_groups + n_b]
    rest = refs[2 + n_groups + n_b :]
    acc_ins = ()
    if has_acc:
        acc_ins, rest = rest[:n_sides], rest[n_sides:]
    outs, rest = rest[:n_sides], rest[n_sides:]
    a_buf, b_buf, acc, a_sem, b_sem, in_sem, out_sem = rest
    depth = a_buf.shape[3]
    row_tiles = int_shape.shape[0]
    strips = ((0, 1), (1, 3), (3, 4), (4, row_tiles))
    window = 2
    followers = {next_pair for _, _, _, next_pair in plan}

    def rows_of(s):
        return pl.ds(strips[s][0] * TILE, (strips[s][1] - strips[s][0]) * TILE)

    def members(pair):
        return (2 * pair, 2 * pair + 1)

    def a_copy(g, s):
        slot, part = plan[g // 2][1], g % 2
        return pltpu.make_async_copy(
            a_refs[g].at[rows_of(s)], a_buf.at[slot, part, rows_of(s)], a_sem.at[slot, part, s]
        )

    def b_copy(j, g, i):
        slot, part = plan[g // 2][1], g % 2
        source = b_refs[b_from[j][sides[i]]]
        if len(source.shape) == 3:
            source = source.at[sides[i]]
        return pltpu.make_async_copy(
            source, b_buf.at[slot, i, pl.ds(part * depth, depth)], b_sem.at[slot, part, i]
        )

    def acc_copy(i, s):
        return pltpu.make_async_copy(
            acc_ins[i].at[rows_of(s)], acc.at[i, rows_of(s)], in_sem.at[i, s]
        )

    def out_copy(i, s):
        return pltpu.make_async_copy(
            acc.at[i, rows_of(s)], outs[i].at[rows_of(s)], out_sem.at[i, s]
        )

    def fetch(pair, s):
        for g in members(pair):
            a_copy(g, s).start()
        if has_acc and pair not in followers:
            for i in range(n_sides):
                acc_copy(i, s).start()

    def begin(pair):
        for g in members(pair):
            for j in range(len(b_spots)):
                @pl.when(meta[b_spots[j]] == meta[spots[g]])
                def _():
                    for i in range(n_sides):
                        b_copy(j, g, i).start()
        for s in range(window):
            fetch(pair, s)

    def guarded(pair, work):
        flag = plan[pair][0]
        if flag is None:
            work()
        else:
            pl.when(meta[1] == flag)(work)

    for pair in range(len(plan)):
        if pair not in followers:
            guarded(pair, functools.partial(begin, pair))

    def multiply(pair):
        _, slot, last, next_pair = plan[pair]
        for g in members(pair):
            for i in range(n_sides):
                b_copy(0, g, i).wait()
        first = [(2 * meta[spots[g]] + meta[0]) * (depth // CHUNK) for g in members(pair)]
        for s in range(len(strips)):
            for g in members(pair):
                a_copy(g, s).wait()
            if has_acc and pair not in followers:
                for i in range(n_sides):
                    acc_copy(i, s).wait()
            if s + window < len(strips):
                fetch(pair, s + window)
            elif s + window == len(strips) and next_pair is not None:
                begin(next_pair)
            for p in range(*strips[s]):
                rows = pl.ds(p * TILE, TILE)
                parts = []
                for h in range(2):
                    for j in range(depth // CHUNK):
                        value = a_buf[slot, h, rows, pl.ds(j * CHUNK, CHUNK)]
                        keep = int_shape[p, (first[h] + j) // 2] != 0
                        parts.append(jnp.where(keep, value, jnp.zeros_like(value)))
                left = jnp.concatenate(parts, axis=1)
                for i in range(n_sides):
                    total = jnp.dot(left, b_buf[slot, i], preferred_element_type=jnp.float32)
                    if has_acc or pair in followers:
                        total = total + acc[i, rows, :]
                    acc[i, rows, :] = total
            if last:
                for i in range(n_sides):
                    out_copy(i, s).start()

    for pair in range(len(plan)):
        guarded(pair, functools.partial(multiply, pair))
    for s in range(len(strips)):
        for i in range(n_sides):
            out_copy(i, s).wait()


def block_matmul(meta, int_shape, groups, b_blocks, sides, plan, weight, accs=()):
    a_refs, spots = [g[0] for g in groups], tuple(g[1] for g in groups)
    b_refs, b_from, b_spots = [], [], []
    for block, spot in b_blocks:
        many = isinstance(block, tuple)
        b_from.append((len(b_refs), len(b_refs) + int(many)))
        b_refs.extend(block if many else (block,))
        b_spots.append(spot)
    rows, depth = a_refs[0].shape
    columns = b_refs[0].shape[-1]
    m = len(sides)
    operands = [meta, int_shape] + a_refs + b_refs + list(accs)
    in_specs = [pl.BlockSpec(memory_space=pltpu.SMEM)] * 2
    in_specs += [pl.BlockSpec(memory_space=pltpu.HBM)] * (len(operands) - 2)
    return pl.pallas_call(
        functools.partial(
            block_kernel, spots, tuple(b_spots), tuple(b_from), plan, sides, bool(accs)
        ),
        out_shape=(jax.ShapeDtypeStruct((rows, columns), jnp.float32),) * m,
        in_specs=in_specs,
        out_specs=(pl.BlockSpec(memory_space=pltpu.HBM),) * m,
        scratch_shapes=[
            pltpu.VMEM((2, 2, rows, depth), jnp.bfloat16),
            pltpu.VMEM((2, m, 2 * depth, columns), jnp.bfloat16),
            pltpu.VMEM((m, rows, columns), jnp.float32),
            pltpu.SemaphoreType.DMA((2, 2, 4)),
            pltpu.SemaphoreType.DMA((2, 2, m)),
            pltpu.SemaphoreType.DMA((m, 4)),
            pltpu.SemaphoreType.DMA((m, 4)),
        ],
        cost_estimate=pl.CostEstimate(
            flops=weight * 2 * rows * depth * columns,
            bytes_accessed=2 * rows * depth,
            transcendentals=0,
        ),
    )(*operands)


def per_device(a, b, int_shape, amp_shape):
    z, ylo, x = lax.axis_index("z"), lax.axis_index("ylo"), lax.axis_index("x")
    yhi, core = lax.axis_index("yhi"), lax.axis_index("core")
    step = sign(core)
    barrier = lax.optimization_barrier

    spots = [x, (x - step) % NX, (x + step) % NX, (x + 2) % NX]
    deep = [z, (z - step) % NZ, (z + step) % NZ, (z + 2) % NZ]
    meta = [core, (ylo == yhi).astype(jnp.int32)]
    meta += [2 * s + yhi for s in spots] + [2 * s + 1 - yhi for s in spots]
    meta += [2 * s + ylo for s in deep] + [2 * s + 1 - ylo for s in deep]
    meta = jnp.stack(meta).astype(jnp.int32)
    first = jnp.stack([core, (2 * z + ylo) * (b.shape[0] // TILE)]).astype(jnp.int32)

    x1 = send(a, X_AHEAD)
    x2 = send(a, X_BACK)
    aq = send(a, Y_FAR)
    shape_t = amp_shape.T
    b0 = masked_half(first, shape_t, send(shape_t, SWAP), b, send(b, SWAP))
    z1 = send(b0, Z_AHEAD)
    z2 = send(b0, Z_BACK)
    q = send(after(b0, aq), Y_NEAR)
    x3 = send(x1, X_AHEAD)
    x5 = send(after(aq, x2), X_BACK)
    z3 = send(after(z1, z2), Z_AHEAD)
    x4 = send(after(aq, x3), X_AHEAD)
    x6 = send(x5, X_BACK)
    z4 = send(after(q, z3), Z_AHEAD)
    z5 = send(after(q, z3), Z_BACK)
    z6 = send(after(z3, q), Y_NEAR)

    a_blocks = [a, x1, x2, x3, aq, x4, x5, x6]
    groups = [(block, 2 + i) for i, block in enumerate(a_blocks)]
    near = [(block, 10 + i) for i, block in enumerate([b0, z1, z2, z3])]
    far = [(block, 14 + i) for i, block in enumerate([q, z4, z5, z6])]
    ready = groups[:4] + [groups[4], groups[6]]
    near_plan = ((1, 0, False, 1), (1, 1, True, None), (0, 0, True, None))
    far_plan = ((0, 0, False, 1), (0, 1, True, None), (1, 0, True, None))
    sums = block_matmul(meta, int_shape, ready, near, (0, 1), near_plan, 2)
    sums = block_matmul(meta, int_shape, ready, far, (0, 1), far_plan, 9, sums)
    late, late_plan = [groups[5], groups[7]], ((None, 0, True, None),)
    theirs = block_matmul(meta, int_shape, late, near + far, (1,), late_plan, 1, sums[1:])[0]
    got = send(theirs, SWAP)
    ours = block_matmul(meta, int_shape, late, near + far, (0,), late_plan, 1, sums[:1])[0]
    return (ours + got).astype(jnp.bfloat16)


def solution(mesh):
    fine = Mesh(mesh.devices.reshape(NZ, 2, NX, 2, 2), AXES)
    row, col = ("z", "ylo"), ("x", "yhi", "core")
    return jax.shard_map(
        per_device,
        mesh=fine,
        in_specs=(P(row, col), P(row, col), P(row, None), P(None, col)),
        out_specs=P(row, col),
        check_vma=False,
    )
```
